32 devices in a mesh: group: 2 (over y), slab: 4 (over z), subj: 2 (over x), yslab: 2 (over core).
Axes of the slice: x: 2, y: 2, z: 4, core: 2. Of those that a mesh axis runs over, the one named last changes fastest.
Arguments:
- subjects: bfloat16 [4, 64, 16, 256], P(('group', 'subj'), 'slab', 'yslab'), parts along dimension 0, may hold values from -6 to 6
- offsets: int32 [4, 3, 64, 16, 256], P(('group', 'subj'), None, 'slab', 'yslab'), parts along dimension 0, may hold values from -2 to 1
- template: float32 [128, 16, 256], P(('group', 'slab'), 'yslab'), parts along dimension 0, may hold values from -6 to 6
- control: float32 [4, 3, 19, 7, 128], P(('group', 'subj')), parts along dimension 0, may hold values from -8 to 8
Outputs:
- template_out: float32 [128, 16, 256], P(('group', 'slab'), 'yslab'), parts along dimension 0
- control_out: float32 [4, 3, 19, 7, 128], P(('group', 'subj')), parts along dimension 0
The draws below stay inside these ranges and needn't reach their ends.
There are 2 independent parts, one for each index of `group`. The reference program is written for one: setup_inputs(seed, part) draws one part's arguments, and reference() takes and returns one part's arrays. A program takes and returns all parts, laid end to end along the dimension named above; each array names one. Nothing has to cross between parts.
All inputs are finite; a program needn't handle non-finite values.
Results may differ from the reference program's by a relative error of at most 0.00065.
Values may be sent and summed in bfloat16 or wider, within the bound.
A program may use at most 64 MiB of HBM per device.

```python
import jax
import jax.numpy as jnp
from jax import lax

NX = 256
KNOT = 4
KNOT_X = 2
HALO = 2
ITERS = 2
NZ = 64
NY = 16
NS = 2
GZ = 19
GY = 7
GX = 128


def plant(array, own_key, least, top_value):
    longest = array.shape.index(max(array.shape))
    spots = []
    for shift in (0, 1):
        where = [jax.random.randint(jax.random.fold_in(own_key, axis), (), 0, length) for axis, length in enumerate(array.shape)]
        where[longest] = (where[longest] + shift) % array.shape[longest]
        spots.append(tuple(where))
    return array.at[spots[0]].set(least).at[spots[1]].set(top_value)


def shard_levels(stream_key, extent, shards, smallest, top_value):
    def one(position, shards_of):
        heights = jax.random.uniform(jax.random.fold_in(jax.random.fold_in(stream_key, 6), position), (shards_of,), jnp.float32, smallest / len(shards), top_value / len(shards))
        return jnp.repeat(jnp.exp(heights), extent[position] // shards_of).reshape((-1,) + (1,) * (len(extent) - position - 1))

    level = one(*shards[0])
    for cut in shards[1:]:
        level = level * one(*cut)
    return level


def bell_draw(stream_key, extent, scale, reach, shards=(), kind=jnp.bfloat16):
    values = jax.random.normal(stream_key, extent, jnp.float32) * scale
    if len(shards) > 0:
        values = shard_levels(stream_key, extent, shards, -0.22, 0.18) * values
    return jnp.clip(values, min=-reach, max=reach).astype(kind)


def setup_inputs(seed: int = 0, part: int = 0) -> dict:
    seeds = jax.random.split(jax.random.key(seed), 5)
    part_keys = jax.random.split(jax.random.fold_in(seeds[4], part), 5)
    return {
        "subjects": bell_draw(part_keys[0], (NS, NZ, NY, NX), 1.0, 6.0, ((0, 2), (1, 4), (2, 2))),
        "offsets": plant(jax.random.randint(part_keys[1], (NS, 3, NZ, NY, NX), -HALO, HALO), jax.random.fold_in(part_keys[1], 1), -HALO, HALO - 1).astype(jnp.int32),
        "template": bell_draw(part_keys[2], (NZ, NY, NX), 1.0, 6.0, ((0, 4), (1, 2)), jnp.float32),
        "control": bell_draw(part_keys[3], (NS, 3, GZ, GY, GX), 2.0, 8.0, ((0, 2),), jnp.float32),
    }


step_length = 0.5
tiny_term = 1e-06

def basis(positions, columns, spacing, wrap):
    cell = positions // spacing
    frac = (positions - cell * spacing).astype(jnp.float32) / spacing
    weights = [(1.0 - frac) ** 3 / 6.0, (3.0 * frac ** 3 - 6.0 * frac ** 2 + 4.0) / 6.0, (-3.0 * frac ** 3 + 3.0 * frac ** 2 + 3.0 * frac + 1.0) / 6.0, frac ** 3 / 6.0]
    index = jnp.arange(columns, dtype=jnp.int32)
    matrix = jnp.zeros((positions.shape[0], columns), jnp.float32)
    for offset in range(4):
        target = cell + offset
        if wrap:
            target = target % columns
        matrix = matrix + jnp.where(index[None, :] == target[:, None], weights[offset][:, None], 0.0)
    return matrix

def forward_field(coeffs, basis_z, basis_y, basis_x):
    high = lax.Precision.HIGHEST
    first = jnp.einsum('cabg,za->czbg', coeffs, basis_z, precision=high)
    second = jnp.einsum('czbg,yb->czyg', first, basis_y, precision=high)
    return jnp.einsum('czyg,xg->czyx', second, basis_x, precision=high)

def adjoint_field(gradient, basis_z, basis_y, basis_x):
    high = lax.Precision.HIGHEST
    first = jnp.einsum('czyx,xg->czyg', gradient, basis_x, precision=high)
    second = jnp.einsum('czyg,yb->czbg', first, basis_y, precision=high)
    return jnp.einsum('czbg,za->cabg', second, basis_z, precision=high)

def trilinear(flat, base_z, base_y, base_x, size_y, size_x, fraction):

    def corner_value(step_z, step_y, step_x):
        index = ((base_z + step_z) * size_y + base_y + step_y) * size_x + base_x + step_x
        return jnp.take(flat, index).astype(jnp.float32)
    frac_z, frac_y, frac_x = (fraction[0], fraction[1], fraction[2])
    along_x = {}
    diff_x = {}
    for step_z in range(2):
        for step_y in range(2):
            low = corner_value(step_z, step_y, 0)
            high = corner_value(step_z, step_y, 1)
            along_x[step_z, step_y] = low * (1.0 - frac_x) + high * frac_x
            diff_x[step_z, step_y] = high - low
    along_y = []
    diff_y = []
    diff_xy = []
    for step_z in range(2):
        along_y.append(along_x[step_z, 0] * (1.0 - frac_y) + along_x[step_z, 1] * frac_y)
        diff_y.append(along_x[step_z, 1] - along_x[step_z, 0])
        diff_xy.append(diff_x[step_z, 0] * (1.0 - frac_y) + diff_x[step_z, 1] * frac_y)
    warped = along_y[0] * (1.0 - frac_z) + along_y[1] * frac_z
    slope_z = along_y[1] - along_y[0]
    slope_y = diff_y[0] * (1.0 - frac_z) + diff_y[1] * frac_z
    slope_x = diff_xy[0] * (1.0 - frac_z) + diff_xy[1] * frac_z
    return (warped, jnp.stack([slope_z, slope_y, slope_x]))

def reference(subjects, offsets, template, control):
    depth, height, width = (subjects.shape[1], subjects.shape[2], subjects.shape[3])
    basis_z = basis(jnp.arange(depth, dtype=jnp.int32), control.shape[2], KNOT, False)
    basis_y = basis(jnp.arange(height, dtype=jnp.int32), control.shape[3], KNOT, False)
    basis_x = basis(jnp.arange(width, dtype=jnp.int32), control.shape[4], KNOT_X, True)
    coord_z = jnp.arange(depth, dtype=jnp.int32)[:, None, None] + HALO
    coord_y = jnp.arange(height, dtype=jnp.int32)[None, :, None] + HALO
    coord_x = jnp.arange(width, dtype=jnp.int32)[None, None, :] + HALO
    size_y = height + 2 * HALO
    size_x = width + 2 * HALO
    current = template
    coeffs_all = control
    for iteration in range(ITERS):

        def per_subject(total, item):
            volume, shifts, coeffs = item
            padded = jnp.pad(volume, HALO).reshape(-1)
            displace = forward_field(coeffs, basis_z, basis_y, basis_x)
            tanh_u = jnp.tanh(displace)
            fraction = 0.5 + 0.5 * tanh_u
            warped, slopes = trilinear(padded, coord_z + shifts[0], coord_y + shifts[1], coord_x + shifts[2], size_y, size_x, fraction)
            resid = warped - current
            grad_u = resid[None] * slopes * (1.0 - tanh_u * tanh_u)
            grid = adjoint_field(grad_u, basis_z, basis_y, basis_x)
            peak = jnp.max(jnp.sqrt(lax.optimization_barrier(jnp.sum(grid * grid, axis=0))))
            updated = coeffs - step_length * grid / (peak + tiny_term)
            return (total + warped, updated)
        total, coeffs_all = lax.scan(per_subject, jnp.zeros(current.shape, jnp.float32), (subjects, offsets, coeffs_all))
        current = total / subjects.shape[0]
    return (current, coeffs_all)
```

```python
import functools

import jax
import jax.numpy as jnp
from jax import lax
from jax.experimental import pallas as pl
from jax.experimental.pallas import tpu as pltpu
from jax.sharding import PartitionSpec as P

KNOT = 4
KNOT_X = 2
HALO = 2
ITERS = 2
SPAN = 2 * HALO + 1
LANES = 128
SUB = 8

step_length = 0.5
tiny_term = 1e-06

MESH = pl.DeviceIdType.MESH


def spline(step, spacing):
    s = step / spacing
    return (
        (1.0 - s) ** 3 / 6.0,
        (3.0 * s**3 - 6.0 * s**2 + 4.0) / 6.0,
        (-3.0 * s**3 + 3.0 * s**2 + 3.0 * s + 1.0) / 6.0,
        s**3 / 6.0,
    )


def spline_table(step, column, spacing, scale):
    out = jnp.zeros(step.shape, jnp.float32)
    for s in range(spacing):
        for k, weight in enumerate(spline(s, spacing)):
            if weight != 0.0:
                out = jnp.where((step == s) & (column == k), jnp.float32(weight * scale), out)
    return out


def pick(values, upper, odd):
    first = jnp.where(upper, values[2], values[0])
    second = jnp.where(upper, values[3], values[1])
    third = jnp.where(upper, values[4], values[2])
    return jnp.where(odd, second, first), jnp.where(odd, third, second)


def split(value):
    high = value.astype(jnp.bfloat16)
    low = (value - high.astype(jnp.float32)).astype(jnp.bfloat16)
    return jnp.concatenate([high, low], axis=1)


def kernel(
    sizes, subj_ref, off_ref, tmpl_ref, ctrl_ref, tout_ref, cout_ref,
    side_ref, face_ref, ext_ref, corner_ref, xw_ref, grad_ref, part_ref, below_ref, above_ref,
    rows_ref, peak_ref, warp_ref,
    side_send, side_recv, face_send, face_recv, part_send, part_recv, edge_send, edge_recv,
    rows_send, rows_recv, last_send, last_recv, peak_send, peak_recv, warp_send, warp_recv,
):
    n_z, n_y, n_s = sizes
    depth, height, width = subj_ref.shape[1:]
    halves = width // LANES
    cells = depth // KNOT
    band = cells + 3
    grid_y, grid_x = ctrl_ref.shape[3:]
    slab = lax.axis_index("slab")
    yslab = lax.axis_index("yslab")
    subj = lax.axis_index("subj")
    first_row = slab * cells

    barrier = pltpu.get_barrier_semaphore()
    for i in range(n_z):
        for k in range(n_y):
            if i or k:
                pl.semaphore_signal(
                    barrier, inc=1, device_id_type=MESH,
                    device_id={"slab": lax.rem(slab + i, n_z), "yslab": lax.rem(yslab + k, n_y)},
                )
    for i in range(1, n_s):
        pl.semaphore_signal(
            barrier, inc=1, device_id={"subj": lax.rem(subj + i, n_s)}, device_id_type=MESH
        )

    def iota(shape, axis):
        return lax.broadcasted_iota(jnp.int32, shape, axis)

    scale_x = 6.0 * KNOT_X**3

    def x_table(shape, x_axis):
        x, g = iota(shape, x_axis), iota(shape, 1 - x_axis)
        column = g - x // KNOT_X
        column = jnp.where(column < 0, column + grid_x, column)
        return spline_table(x % KNOT_X, column, KNOT_X, scale_x).astype(jnp.bfloat16)

    spread_x = x_table((grid_x, width), 1)
    spread_x = jnp.concatenate([spread_x, spread_x], axis=0)
    gather_x = x_table((width, grid_x), 0)
    gather_x = jnp.concatenate([gather_x, gather_x], axis=0)

    def y_weights(y, b):
        column = b - (yslab * height + y) // KNOT
        return spline_table(y % KNOT, column, KNOT, 1.0 / scale_x)

    rows8 = iota((SUB, LANES), 0)
    spread_y = [y_weights(rows8, (rows8 - d) % SUB) for d in range(SUB)]
    gather_y = [y_weights((rows8 - d) % SUB, rows8) for d in range(SUB)]

    def turn(value, weights):
        total = value * weights[0][None]
        for d in range(1, SUB):
            total = total + pltpu.roll(value, d, 1) * weights[d][None]
        return total

    def forward(tiles):
        mixed = turn(tiles, spread_y).reshape(band * 3 * SUB, LANES)
        out = jnp.dot(split(mixed), spread_x, preferred_element_type=jnp.float32)
        return out.reshape(band * 3, SUB, width)

    def adjoint(tiles):
        out = jnp.dot(
            split(tiles.reshape(band * 3 * SUB, width)), gather_x, preferred_element_type=jnp.float32
        )
        return turn(out.reshape(band * 3, SUB, LANES), gather_y)

    @pl.when(slab == 0)
    def _():
        below_ref[...] = jnp.zeros_like(below_ref)

    @pl.when(slab == n_z - 1)
    def _():
        above_ref[...] = jnp.zeros_like(above_ref)

    pl.semaphore_wait(barrier, n_z * n_y - 1 + n_s - 1)

    def inside(dz, dy):
        z, y = slab + dz, yslab + dy
        return (z >= 0) & (z < n_z) & (y >= 0) & (y < n_y)

    moves = []
    for dy in (-1, 1):
        moves.append((0, dy, pltpu.make_async_remote_copy(
            src_ref=subj_ref.at[0], dst_ref=side_ref.at[(1 - dy) // 2],
            send_sem=side_send.at[(1 - dy) // 2], recv_sem=side_recv.at[(1 - dy) // 2],
            device_id={"yslab": yslab + dy}, device_id_type=MESH)))
    for dz in (-1, 1):
        start = 0 if dz < 0 else depth - HALO
        for dy in (-1, 0, 1):
            a, b = (1 - dz) // 2, 1 - dy
            moves.append((dz, dy, pltpu.make_async_remote_copy(
                src_ref=subj_ref.at[0, pl.ds(start, HALO)], dst_ref=face_ref.at[a, b],
                send_sem=face_send.at[a, b], recv_sem=face_recv.at[a, b],
                device_id={"slab": slab + dz, "yslab": yslab + dy}, device_id_type=MESH)))
    for dz, dy, copy in moves:
        pl.when(inside(dz, dy))(copy.start)

    pad = jnp.zeros((SUB - grid_y, LANES), jnp.float32)
    tiles = jnp.stack([
        jnp.concatenate([ctrl_ref[0, c, first_row + a], pad], axis=0)
        for a in range(band) for c in range(3)
    ])
    xw_ref[...] = forward(tiles)

    lane = iota((1, SUB, LANES), 2)

    def place(z, tile, block):
        planes = block.shape[0]
        parts = [block[:, :, h * LANES:(h + 1) * LANES] for h in range(halves)]
        zero = jnp.zeros_like(parts[0])
        for dx in range(-HALO, HALO + 1):
            if dx == 0:
                moved = parts
            else:
                rolled = [pltpu.roll(p, (-dx) % LANES, 2) for p in parts]
                moved = []
                for h in range(halves):
                    other = h + (1 if dx > 0 else -1)
                    fill = rolled[other] if 0 <= other < halves else zero
                    edge = lane >= LANES - dx if dx > 0 else lane < -dx
                    moved.append(jnp.where(edge, fill, rolled[h]))
            for h in range(halves):
                ext_ref[dx + HALO, h, pl.ds(z, planes), tile * SUB:(tile + 1) * SUB, :] = moved[h]

    own = 4

    def place_many(tile, load):
        def body(i, carry):
            place(HALO + i * own, tile, load(pl.ds(i * own, own)).astype(jnp.float32))
            return carry
        lax.fori_loop(0, depth // own, body, 0)

    place_many(1, lambda part: subj_ref[0, part])

    for dz, dy, copy in moves:
        pl.when(inside(-dz, -dy))(copy.wait_recv)
    for d, dy in enumerate((-1, 1)):
        tile = 1 + dy

        @pl.when(inside(0, dy))
        def _():
            place_many(tile, lambda part: side_ref[d, part])

        @pl.when(jnp.logical_not(inside(0, dy)))
        def _():
            ext_ref[:, :, :, tile * SUB:(tile + 1) * SUB, :] = jnp.zeros(
                (SPAN, halves, depth + 2 * HALO, SUB, LANES), jnp.float32)
    for a, dz in enumerate((-1, 1)):
        z = 0 if dz < 0 else depth + HALO
        for b, dy in enumerate((-1, 0, 1)):
            @pl.when(inside(dz, dy))
            def _():
                place(z, b, face_ref[a, b].astype(jnp.float32))

            @pl.when(jnp.logical_not(inside(dz, dy)))
            def _():
                ext_ref[:, :, z:z + HALO, b * SUB:(b + 1) * SUB, :] = jnp.zeros(
                    (SPAN, halves, HALO, SUB, LANES), jnp.float32)

    def corners(z, carry):
        for h in range(halves):
            cut = slice(h * LANES, (h + 1) * LANES)
            bits = [(off_ref[0, i, z, :, cut] >= 0, (off_ref[0, i, z, :, cut] & 1) == 1) for i in range(3)]
            by_z = []
            for dz in range(SPAN):
                by_y = []
                for dy in range(SPAN):
                    start = SUB - HALO + dy
                    row = [ext_ref[dx, h, z + dz, start:start + SUB, :] for dx in range(SPAN)]
                    by_y.append(pick(row, *bits[2]))
                by_z.append([pick([v[x] for v in by_y], *bits[1]) for x in range(2)])
            for x in range(2):
                for y in range(2):
                    low, high = pick([v[x][y] for v in by_z], *bits[0])
                    corner_ref[0 + 2 * y + x, z, :, cut] = low
                    corner_ref[4 + 2 * y + x, z, :, cut] = high
        return carry

    lax.fori_loop(0, depth, corners, 0)

    weights_z = [spline(s, KNOT) for s in range(KNOT)]
    sends = [(inside(dz, dy), copy) for dz, dy, copy in moves]
    late = []
    warp_copies = []

    for it in range(ITERS):
        grad_ref[...] = jnp.zeros_like(grad_ref)
        if it > 0:
            for copy in warp_copies[-1]:
                copy.wait_recv()

        def cell(j, carry):
            for h in range(halves):
                cut = slice(h * LANES, (h + 1) * LANES)
                knots = [[xw_ref[(j + k) * 3 + c, :, cut] for k in range(4)] for c in range(3)]
                sums = [[None] * 4 for _ in range(3)]
                for s in range(KNOT):
                    z = j * KNOT + s
                    used = [k for k in range(4) if weights_z[s][k] != 0.0]
                    th, f = [], []
                    for c in range(3):
                        u = sum(knots[c][k] * weights_z[s][k] for k in used)
                        th.append(jnp.tanh(u))
                        f.append(0.5 + 0.5 * th[c])
                    v = [corner_ref[i, z, :, cut] for i in range(8)]
                    dx = [v[2 * i + 1] - v[2 * i] for i in range(4)]
                    ax = [v[2 * i] + dx[i] * f[2] for i in range(4)]
                    dy = [ax[1] - ax[0], ax[3] - ax[2]]
                    ay = [ax[0] + dy[0] * f[1], ax[2] + dy[1] * f[1]]
                    dxy = [dx[0] + (dx[1] - dx[0]) * f[1], dx[2] + (dx[3] - dx[2]) * f[1]]
                    slope_z = ay[1] - ay[0]
                    warped = ay[0] + slope_z * f[0]
                    slope_y = dy[0] + (dy[1] - dy[0]) * f[0]
                    slope_x = dxy[0] + (dxy[1] - dxy[0]) * f[0]
                    warp_ref[it, subj, z, :, cut] = warped
                    if it == 0:
                        current = tmpl_ref[z, :, cut]
                    else:
                        current = sum(warp_ref[it - 1, i, z, :, cut] for i in range(n_s)) * (1.0 / n_s)
                    resid = warped - current
                    for c, slope in enumerate((slope_z, slope_y, slope_x)):
                        g = resid * slope * (1.0 - th[c] * th[c])
                        for k in used:
                            term = g * weights_z[s][k]
                            sums[c][k] = term if sums[c][k] is None else sums[c][k] + term
                for c in range(3):
                    for k in range(4):
                        grad_ref[(j + k) * 3 + c, :, cut] += sums[c][k]
            return carry

        lax.fori_loop(0, cells, cell, 0)

        copies = []
        for i in range(1, n_s):
            copy = pltpu.make_async_remote_copy(
                src_ref=warp_ref.at[it, subj], dst_ref=warp_ref.at[it, subj],
                send_sem=warp_send.at[it, i], recv_sem=warp_recv.at[it, i],
                device_id={"subj": lax.rem(subj + i, n_s)}, device_id_type=MESH)
            copies.append(copy)
        warp_copies.append(copies)

        part = adjoint(grad_ref[...])
        part_ref[it, yslab] = part.reshape(band, 3, SUB, LANES).astype(jnp.bfloat16)

        part_copies = []
        for i in range(1, n_y):
            copy = pltpu.make_async_remote_copy(
                src_ref=part_ref.at[it, yslab], dst_ref=part_ref.at[it, yslab],
                send_sem=part_send.at[it, i], recv_sem=part_recv.at[it, i],
                device_id={"yslab": lax.rem(yslab + i, n_y)}, device_id_type=MESH)
            part_copies.append(copy)
        edge_copies = []
        for e, dz in enumerate((1, -1)):
            landing = below_ref if dz > 0 else above_ref
            start = cells if dz > 0 else 0
            for i in range(n_y):
                copy = pltpu.make_async_remote_copy(
                    src_ref=part_ref.at[it, yslab, pl.ds(start, 3)], dst_ref=landing.at[it, yslab],
                    send_sem=edge_send.at[it, e, i], recv_sem=edge_recv.at[it, e, i],
                    device_id={"slab": slab + dz, "yslab": lax.rem(yslab + i, n_y)},
                    device_id_type=MESH)
                edge_copies.append((inside(dz, 0), inside(-dz, 0), copy))
        for go, _, copy in edge_copies:
            pl.when(go)(copy.start)
        for copy in part_copies:
            copy.start()
        for copy in copies:
            copy.start()
        for copy in part_copies:
            copy.wait_recv()
        for _, come, copy in edge_copies:
            pl.when(come)(copy.wait_recv)
        sends += [(go, copy) for go, _, copy in edge_copies]
        sends += [(None, copy) for copy in part_copies + copies]

        def over_y(ref, where):
            return sum(ref[it, k, where].astype(jnp.float32) for k in range(n_y))

        rows = []
        for a in range(band):
            row = over_y(part_ref, a)
            if a < 3:
                row = row + over_y(below_ref, a)
            if a >= cells:
                row = row + over_y(above_ref, a - cells)
            rows.append(row)
        square = None
        for row in rows:
            here = row[0] * row[0] + row[1] * row[1] + row[2] * row[2]
            square = here if square is None else jnp.maximum(square, here)
        peak_ref[it, slab] = square
        peak_copies = []
        for i in range(1, n_z):
            copy = pltpu.make_async_remote_copy(
                src_ref=peak_ref.at[it, slab], dst_ref=peak_ref.at[it, slab],
                send_sem=peak_send.at[it, i], recv_sem=peak_recv.at[it, i],
                device_id={"slab": lax.rem(slab + i, n_z)}, device_id_type=MESH)
            peak_copies.append(copy)
        for a in range(cells):
            rows_ref[it, first_row + a] = rows[a].astype(jnp.bfloat16)

        @pl.when(slab == n_z - 1)
        def _():
            for a in range(cells, band):
                rows_ref[it, first_row + a] = rows[a].astype(jnp.bfloat16)

        for copy in peak_copies:
            copy.start()
        last = n_z * cells
        for i in range(1, n_z):
            target = {"slab": lax.rem(slab + i, n_z)}
            own_rows = rows_ref.at[it, pl.ds(first_row, cells)]
            copy = pltpu.make_async_remote_copy(
                src_ref=own_rows, dst_ref=own_rows,
                send_sem=rows_send.at[it, i], recv_sem=rows_recv.at[it, i],
                device_id=target, device_id_type=MESH)
            copy.start()
            late.append((None, copy))
            sends.append((None, copy))
            last_rows = rows_ref.at[it, pl.ds(last, 3)]
            copy = pltpu.make_async_remote_copy(
                src_ref=last_rows, dst_ref=last_rows,
                send_sem=last_send.at[it, i], recv_sem=last_recv.at[it, i],
                device_id=target, device_id_type=MESH)
            pl.when(slab == n_z - 1)(copy.start)
            late.append((lax.rem(slab - i + n_z, n_z) == n_z - 1, copy))
            sends.append((slab == n_z - 1, copy))
        sends += [(None, copy) for copy in peak_copies]

        if it + 1 < ITERS:
            change = forward(jnp.concatenate(rows, axis=0))
        for copy in peak_copies:
            copy.wait_recv()
        if it + 1 < ITERS:
            top = peak_ref[it, 0]
            for k in range(1, n_z):
                top = jnp.maximum(top, peak_ref[it, k])
            top = jnp.sqrt(jnp.max(top, axis=(0, 1), keepdims=True))
            rate = step_length / (top + tiny_term)
            xw_ref[...] = xw_ref[...] - change * rate[None]

    for copy in warp_copies[-1]:
        copy.wait_recv()
    tout_ref[...] = sum(warp_ref[ITERS - 1, i] for i in range(n_s)) * (1.0 / n_s)

    rates = []
    for it in range(ITERS):
        top = peak_ref[it, 0]
        for k in range(1, n_z):
            top = jnp.maximum(top, peak_ref[it, k])
        top = jnp.sqrt(jnp.max(top, axis=(0, 1), keepdims=True))
        rates.append(step_length / (top + tiny_term))
    for come, copy in late:
        if come is None:
            copy.wait_recv()
        else:
            pl.when(come)(copy.wait_recv)
    for a in range(cout_ref.shape[2]):
        steps = [rows_ref[it, a].astype(jnp.float32) * rates[it][None] for it in range(ITERS)]
        for c in range(3):
            value = ctrl_ref[0, c, a]
            for it in range(ITERS):
                value = value - steps[it][c, :grid_y]
            cout_ref[0, c, a] = value
    for go, copy in sends:
        if go is None:
            copy.wait_send()
        else:
            pl.when(go)(copy.wait_send)


def shards(sizes, subjects, offsets, template, control):
    n_z, n_y, n_s = sizes
    depth, height, width = subjects.shape[1:]
    halves = width // LANES
    cells = depth // KNOT
    band = cells + 3
    grid_z = control.shape[2]
    low, full = jnp.bfloat16, jnp.float32
    dma = pltpu.SemaphoreType.DMA
    scratch = [
        pltpu.VMEM((2, depth, height, width), low),
        pltpu.VMEM((2, 3, HALO, height, width), low),
        pltpu.VMEM((SPAN, halves, depth + 2 * HALO, 3 * SUB, LANES), full),
        pltpu.VMEM((8, depth, height, width), full),
        pltpu.VMEM((band * 3, SUB, width), full),
        pltpu.VMEM((band * 3, SUB, width), full),
        pltpu.VMEM((ITERS, n_y, band, 3, SUB, LANES), low),
        pltpu.VMEM((ITERS, n_y, 3, 3, SUB, LANES), low),
        pltpu.VMEM((ITERS, n_y, 3, 3, SUB, LANES), low),
        pltpu.VMEM((ITERS, grid_z, 3, SUB, LANES), low),
        pltpu.VMEM((ITERS, n_z, SUB, LANES), full),
        pltpu.VMEM((ITERS, n_s, depth, height, width), full),
        dma((2,)), dma((2,)), dma((2, 3)), dma((2, 3)),
        dma((ITERS, n_y)), dma((ITERS, n_y)), dma((ITERS, 2, n_y)), dma((ITERS, 2, n_y)),
        dma((ITERS, n_z)), dma((ITERS, n_z)), dma((ITERS, n_z)), dma((ITERS, n_z)),
        dma((ITERS, n_z)), dma((ITERS, n_z)), dma((ITERS, n_s)), dma((ITERS, n_s)),
    ]
    return pl.pallas_call(
        functools.partial(kernel, sizes),
        out_shape=(
            jax.ShapeDtypeStruct(template.shape, full),
            jax.ShapeDtypeStruct(control.shape, full),
        ),
        in_specs=[pl.BlockSpec(memory_space=pltpu.VMEM)] * 4,
        out_specs=(pl.BlockSpec(memory_space=pltpu.VMEM),) * 2,
        scratch_shapes=scratch,
        compiler_params=pltpu.CompilerParams(collective_id=0, has_side_effects=True),
        name="register",
    )(subjects, offsets, template, control)


def solution(mesh):
    in_specs = (
        P(("group", "subj"), "slab", "yslab", None),
        P(("group", "subj"), None, "slab", "yslab", None),
        P(("group", "slab"), "yslab", None),
        P(("group", "subj"), None, None, None, None),
    )
    out_specs = (P(("group", "slab"), "yslab", None), P(("group", "subj"), None, None, None, None))
    sizes = (mesh.shape["slab"], mesh.shape["yslab"], mesh.shape["subj"])
    body = functools.partial(shards, sizes)
    return jax.shard_map(body, mesh=mesh, in_specs=in_specs, out_specs=out_specs, check_vma=False)
```

```python
import functools

import jax
import jax.numpy as jnp
from jax import lax
from jax.experimental import pallas as pl
from jax.experimental.pallas import tpu as pltpu
from jax.sharding import PartitionSpec as P

KNOT = 4
KNOT_X = 2
HALO = 2
ITERS = 2
SPAN = 2 * HALO + 1
LANES = 128
SUB = 8

step_length = 0.5
tiny_term = 1e-06

MESH = pl.DeviceIdType.MESH


def spline(step, spacing):
    s = step / spacing
    return (
        (1.0 - s) ** 3 / 6.0,
        (3.0 * s**3 - 6.0 * s**2 + 4.0) / 6.0,
        (-3.0 * s**3 + 3.0 * s**2 + 3.0 * s + 1.0) / 6.0,
        s**3 / 6.0,
    )


def spline_table(step, column, spacing, scale):
    out = jnp.zeros(step.shape, jnp.float32)
    for s in range(spacing):
        for k, weight in enumerate(spline(s, spacing)):
            if weight != 0.0:
                out = jnp.where((step == s) & (column == k), jnp.float32(weight * scale), out)
    return out


def pick(values, upper, odd):
    first = jnp.where(upper, values[2], values[0])
    second = jnp.where(upper, values[3], values[1])
    third = jnp.where(upper, values[4], values[2])
    return jnp.where(odd, second, first), jnp.where(odd, third, second)


def split(value):
    high = value.astype(jnp.bfloat16)
    low = (value - high.astype(jnp.float32)).astype(jnp.bfloat16)
    return jnp.concatenate([high, low], axis=1)


def kernel(
    sizes, subj_hbm, off_hbm, tmpl_hbm, ctrl_hbm, tout_hbm, cout_hbm,
    subj_ref, off_ref, tmpl_ref, ctrl_ref, tout_ref, cout_ref, base_ref,
    side_ref, face_ref, ext_ref, corner_ref, xw_ref, grad_ref, part_ref, below_ref, above_ref,
    rows_ref, peak_ref, warp_ref,
    side_send, side_recv, face_send, face_recv, part_send, part_recv, edge_send, edge_recv,
    rows_send, rows_recv, last_send, last_recv, peak_send, peak_recv, warp_send, warp_recv,
    relay_sem, load_sem, store_sem,
):
    n_z, n_y, n_s = sizes
    depth, height, width = subj_ref.shape[1:]
    halves = width // LANES
    cells = depth // KNOT
    band = cells + 3
    grid_z, grid_y, grid_x = ctrl_ref.shape[1], ctrl_ref.shape[2], ctrl_ref.shape[4]
    slab = lax.axis_index("slab")
    yslab = lax.axis_index("yslab")
    subj = lax.axis_index("subj")
    first_row = slab * cells

    def inside(dz, dy):
        z, y = slab + dz, yslab + dy
        return (z >= 0) & (z < n_z) & (y >= 0) & (y < n_y)

    barrier = pltpu.get_barrier_semaphore()
    for k in range(1, n_y):
        pl.semaphore_signal(
            barrier, inc=1, device_id={"yslab": lax.rem(yslab + k, n_y)}, device_id_type=MESH
        )
    for i in range(1, n_s):
        pl.semaphore_signal(
            barrier, inc=1, device_id={"subj": lax.rem(subj + i, n_s)}, device_id_type=MESH
        )
    greeted = n_y - 1 + n_s - 1
    for dz in (-1, 1):
        @pl.when(inside(dz, 0))
        def _():
            for k in range(n_y):
                pl.semaphore_signal(
                    barrier, inc=1, device_id_type=MESH,
                    device_id={"slab": slab + dz, "yslab": lax.rem(yslab + k, n_y)},
                )
        greeted = greeted + jnp.where(inside(dz, 0), n_y, 0)

    loads = [
        pltpu.make_async_copy(src, dst, load_sem.at[i])
        for i, (src, dst) in enumerate((
            (subj_hbm, subj_ref), (ctrl_hbm, ctrl_ref), (off_hbm, off_ref), (tmpl_hbm, tmpl_ref)))
    ]
    for load in loads:
        load.start()

    def iota(shape, axis):
        return lax.broadcasted_iota(jnp.int32, shape, axis)

    scale_x = 6.0 * KNOT_X**3

    def x_table(shape, x_axis):
        x, g = iota(shape, x_axis), iota(shape, 1 - x_axis)
        column = g - x // KNOT_X
        column = jnp.where(column < 0, column + grid_x, column)
        return spline_table(x % KNOT_X, column, KNOT_X, scale_x).astype(jnp.bfloat16)

    spread_x = x_table((grid_x, width), 1)
    spread_x = jnp.concatenate([spread_x, spread_x], axis=0)
    gather_x = x_table((width, grid_x), 0)
    gather_x = jnp.concatenate([gather_x, gather_x], axis=0)

    def y_weights(y, b):
        column = b - (yslab * height + y) // KNOT
        return spline_table(y % KNOT, column, KNOT, 1.0 / scale_x)

    rows8 = iota((SUB, LANES), 0)
    spread_y = [y_weights(rows8, (rows8 - d) % SUB) for d in range(SUB)]
    gather_y = [y_weights((rows8 - d) % SUB, rows8) for d in range(SUB)]

    def turn(value, weights):
        total = value * weights[0][None]
        for d in range(1, SUB):
            total = total + pltpu.roll(value, d, 1) * weights[d][None]
        return total

    def forward(tiles):
        mixed = turn(tiles, spread_y).reshape(band * 3 * SUB, LANES)
        out = jnp.dot(split(mixed), spread_x, preferred_element_type=jnp.float32)
        return out.reshape(band * 3, SUB, width)

    def adjoint(tiles):
        out = jnp.dot(
            split(tiles.reshape(band * 3 * SUB, width)), gather_x, preferred_element_type=jnp.float32
        )
        return turn(out.reshape(band * 3, SUB, LANES), gather_y)

    @pl.when(slab == 0)
    def _():
        below_ref[...] = jnp.zeros_like(below_ref)

    @pl.when(slab == n_z - 1)
    def _():
        above_ref[...] = jnp.zeros_like(above_ref)

    loads[0].wait()
    pl.semaphore_wait(barrier, greeted)

    def relay_signal():
        for d, dz in enumerate((-1, 1)):
            @pl.when(inside(dz, 0))
            def _():
                pl.semaphore_signal(
                    relay_sem.at[d], inc=1, device_id={"slab": slab + dz}, device_id_type=MESH
                )

    def relay_wait():
        for d, dz in enumerate((1, -1)):
            @pl.when(inside(dz, 0))
            def _():
                pl.semaphore_wait(relay_sem.at[d], 1)

    moves = []
    for dy in (-1, 1):
        moves.append((0, dy, pltpu.make_async_remote_copy(
            src_ref=subj_ref.at[0], dst_ref=side_ref.at[(1 - dy) // 2],
            send_sem=side_send.at[(1 - dy) // 2], recv_sem=side_recv.at[(1 - dy) // 2],
            device_id={"yslab": yslab + dy}, device_id_type=MESH)))
    for dz in (-1, 1):
        start = 0 if dz < 0 else depth - HALO
        for dy in (-1, 0, 1):
            a, b = (1 - dz) // 2, 1 - dy
            moves.append((dz, dy, pltpu.make_async_remote_copy(
                src_ref=subj_ref.at[0, pl.ds(start, HALO)], dst_ref=face_ref.at[a, b],
                send_sem=face_send.at[a, b], recv_sem=face_recv.at[a, b],
                device_id={"slab": slab + dz, "yslab": yslab + dy}, device_id_type=MESH)))
    for dz, dy, copy in moves:
        pl.when(inside(dz, dy))(copy.start)
    if n_z > 2:
        relay_signal()
    loads[1].wait()

    pad = jnp.zeros((SUB - grid_y, LANES), jnp.float32)
    tiles = jnp.stack([
        jnp.concatenate([ctrl_ref[c, first_row + a, :, 0, :], pad], axis=0)
        for a in range(band) for c in range(3)
    ])
    xw_ref[...] = forward(tiles)

    lane = iota((1, SUB, LANES), 2)

    def place(z, tile, block):
        planes = block.shape[0]
        parts = [block[:, :, h * LANES:(h + 1) * LANES] for h in range(halves)]
        zero = jnp.zeros_like(parts[0])
        for dx in range(-HALO, HALO + 1):
            if dx == 0:
                moved = parts
            else:
                rolled = [pltpu.roll(p, (-dx) % LANES, 2) for p in parts]
                moved = []
                for h in range(halves):
                    other = h + (1 if dx > 0 else -1)
                    fill = rolled[other] if 0 <= other < halves else zero
                    edge = lane >= LANES - dx if dx > 0 else lane < -dx
                    moved.append(jnp.where(edge, fill, rolled[h]))
            for h in range(halves):
                ext_ref[dx + HALO, h, pl.ds(z, planes), tile * SUB:(tile + 1) * SUB, :] = moved[h]

    own = 4

    def place_many(tile, load):
        def body(i, carry):
            place(HALO + i * own, tile, load(pl.ds(i * own, own)).astype(jnp.float32))
            return carry
        lax.fori_loop(0, depth // own, body, 0)

    place_many(1, lambda part: subj_ref[0, part])

    for dz, dy, copy in moves:
        if dz == 0:
            pl.when(inside(-dz, -dy))(copy.wait_recv)
    for d, dy in enumerate((-1, 1)):
        tile = 1 + dy

        @pl.when(inside(0, dy))
        def _():
            place_many(tile, lambda part: side_ref[d, part])

        @pl.when(jnp.logical_not(inside(0, dy)))
        def _():
            ext_ref[:, :, :, tile * SUB:(tile + 1) * SUB, :] = jnp.zeros(
                (SPAN, halves, depth + 2 * HALO, SUB, LANES), jnp.float32)
    def corners(z, carry):
        for h in range(halves):
            cut = slice(h * LANES, (h + 1) * LANES)
            bits = [(off_ref[0, i, z, :, cut] >= 0, (off_ref[0, i, z, :, cut] & 1) == 1) for i in range(3)]
            by_z = []
            for dz in range(SPAN):
                by_y = []
                for dy in range(SPAN):
                    start = SUB - HALO + dy
                    row = [ext_ref[dx, h, z + dz, start:start + SUB, :] for dx in range(SPAN)]
                    by_y.append(pick(row, *bits[2]))
                by_z.append([pick([v[x] for v in by_y], *bits[1]) for x in range(2)])
            for x in range(2):
                for y in range(2):
                    low, high = pick([v[x][y] for v in by_z], *bits[0])
                    corner_ref[0 + 2 * y + x, z, :, cut] = low
                    corner_ref[4 + 2 * y + x, z, :, cut] = high
        return carry

    loads[2].wait()
    lax.fori_loop(HALO, depth - HALO, corners, 0)
    for dz, dy, copy in moves:
        if dz != 0:
            pl.when(inside(-dz, -dy))(copy.wait_recv)
    for a, dz in enumerate((-1, 1)):
        z = 0 if dz < 0 else depth + HALO
        for b, dy in enumerate((-1, 0, 1)):
            @pl.when(inside(dz, dy))
            def _():
                place(z, b, face_ref[a, b].astype(jnp.float32))

            @pl.when(jnp.logical_not(inside(dz, dy)))
            def _():
                ext_ref[:, :, z:z + HALO, b * SUB:(b + 1) * SUB, :] = jnp.zeros(
                    (SPAN, halves, HALO, SUB, LANES), jnp.float32)
    lax.fori_loop(0, HALO, corners, 0)
    lax.fori_loop(depth - HALO, depth, corners, 0)
    for _ in range(2, n_z - 1):
        relay_wait()
        relay_signal()
    loads[3].wait()

    weights_z = [spline(s, KNOT) for s in range(KNOT)]
    sends = [(inside(dz, dy), copy) for dz, dy, copy in moves]
    late = []
    warp_copies = []
    rates = []

    for it in range(ITERS):
        grad_ref[...] = jnp.zeros_like(grad_ref)
        if it > 0:
            for copy in warp_copies[-1]:
                copy.wait_recv()

        def cell(j, carry):
            for h in range(halves):
                cut = slice(h * LANES, (h + 1) * LANES)
                knots = [[xw_ref[(j + k) * 3 + c, :, cut] for k in range(4)] for c in range(3)]
                sums = [[None] * 4 for _ in range(3)]
                for s in range(KNOT):
                    z = j * KNOT + s
                    used = [k for k in range(4) if weights_z[s][k] != 0.0]
                    th, f = [], []
                    for c in range(3):
                        u = sum(knots[c][k] * weights_z[s][k] for k in used)
                        th.append(jnp.tanh(u))
                        f.append(0.5 + 0.5 * th[c])
                    v = [corner_ref[i, z, :, cut] for i in range(8)]
                    dx = [v[2 * i + 1] - v[2 * i] for i in range(4)]
                    ax = [v[2 * i] + dx[i] * f[2] for i in range(4)]
                    dy = [ax[1] - ax[0], ax[3] - ax[2]]
                    ay = [ax[0] + dy[0] * f[1], ax[2] + dy[1] * f[1]]
                    dxy = [dx[0] + (dx[1] - dx[0]) * f[1], dx[2] + (dx[3] - dx[2]) * f[1]]
                    slope_z = ay[1] - ay[0]
                    warped = ay[0] + slope_z * f[0]
                    slope_y = dy[0] + (dy[1] - dy[0]) * f[0]
                    slope_x = dxy[0] + (dxy[1] - dxy[0]) * f[0]
                    warp_ref[it, subj, z, :, cut] = warped
                    if it == 0:
                        current = tmpl_ref[z, :, cut]
                    else:
                        current = sum(warp_ref[it - 1, i, z, :, cut] for i in range(n_s)) * (1.0 / n_s)
                    resid = warped - current
                    for c, slope in enumerate((slope_z, slope_y, slope_x)):
                        g = resid * slope * (1.0 - th[c] * th[c])
                        for k in used:
                            term = g * weights_z[s][k]
                            sums[c][k] = term if sums[c][k] is None else sums[c][k] + term
                for c in range(3):
                    for k in range(4):
                        grad_ref[(j + k) * 3 + c, :, cut] += sums[c][k]
            return carry

        lax.fori_loop(0, cells, cell, 0)

        copies = []
        for i in range(1, n_s):
            copy = pltpu.make_async_remote_copy(
                src_ref=warp_ref.at[it, subj], dst_ref=warp_ref.at[it, subj],
                send_sem=warp_send.at[it, i], recv_sem=warp_recv.at[it, i],
                device_id={"subj": lax.rem(subj + i, n_s)}, device_id_type=MESH)
            copies.append(copy)
        warp_copies.append(copies)

        part = adjoint(grad_ref[...])
        part_ref[it, yslab] = part.reshape(band, 3, SUB, LANES).astype(jnp.bfloat16)

        part_copies = []
        for i in range(1, n_y):
            copy = pltpu.make_async_remote_copy(
                src_ref=part_ref.at[it, yslab], dst_ref=part_ref.at[it, yslab],
                send_sem=part_send.at[it, i], recv_sem=part_recv.at[it, i],
                device_id={"yslab": lax.rem(yslab + i, n_y)}, device_id_type=MESH)
            part_copies.append(copy)
        edge_copies = []
        for e, dz in enumerate((1, -1)):
            landing = below_ref if dz > 0 else above_ref
            start = cells if dz > 0 else 0
            for i in range(n_y):
                copy = pltpu.make_async_remote_copy(
                    src_ref=part_ref.at[it, yslab, pl.ds(start, 3)], dst_ref=landing.at[it, yslab],
                    send_sem=edge_send.at[it, e, i], recv_sem=edge_recv.at[it, e, i],
                    device_id={"slab": slab + dz, "yslab": lax.rem(yslab + i, n_y)},
                    device_id_type=MESH)
                edge_copies.append((inside(dz, 0), inside(-dz, 0), copy))
        for go, _, copy in edge_copies:
            pl.when(go)(copy.start)
        for copy in part_copies:
            copy.start()
        for copy in copies:
            copy.start()
        for copy in part_copies:
            copy.wait_recv()
        for _, come, copy in edge_copies:
            pl.when(come)(copy.wait_recv)
        sends += [(go, copy) for go, _, copy in edge_copies]
        sends += [(None, copy) for copy in part_copies + copies]

        def over_y(ref, where):
            return sum(ref[it, k, where].astype(jnp.float32) for k in range(n_y))

        rows = []
        for a in range(band):
            row = over_y(part_ref, a)
            if a < 3:
                row = row + over_y(below_ref, a)
            if a >= cells:
                row = row + over_y(above_ref, a - cells)
            rows.append(row)
        square = None
        for row in rows:
            here = row[0] * row[0] + row[1] * row[1] + row[2] * row[2]
            square = here if square is None else jnp.maximum(square, here)
        peak_ref[it, slab] = square
        if it == 0 and n_z > 2:
            relay_wait()
        peak_copies = []
        for i in range(1, n_z):
            copy = pltpu.make_async_remote_copy(
                src_ref=peak_ref.at[it, slab], dst_ref=peak_ref.at[it, slab],
                send_sem=peak_send.at[it, i], recv_sem=peak_recv.at[it, i],
                device_id={"slab": lax.rem(slab + i, n_z)}, device_id_type=MESH)
            peak_copies.append(copy)
        for a in range(cells):
            rows_ref[it, first_row + a] = rows[a].astype(jnp.bfloat16)

        @pl.when(slab == n_z - 1)
        def _():
            for a in range(cells, band):
                rows_ref[it, first_row + a] = rows[a].astype(jnp.bfloat16)

        for copy in peak_copies:
            copy.start()
        last = n_z * cells
        for i in range(1, n_z):
            target = {"slab": lax.rem(slab + i, n_z)}
            own_rows = rows_ref.at[it, pl.ds(first_row, cells)]
            copy = pltpu.make_async_remote_copy(
                src_ref=own_rows, dst_ref=own_rows,
                send_sem=rows_send.at[it, i], recv_sem=rows_recv.at[it, i],
                device_id=target, device_id_type=MESH)
            copy.start()
            late.append((it, None, copy))
            sends.append((None, copy))
            last_rows = rows_ref.at[it, pl.ds(last, 3)]
            copy = pltpu.make_async_remote_copy(
                src_ref=last_rows, dst_ref=last_rows,
                send_sem=last_send.at[it, i], recv_sem=last_recv.at[it, i],
                device_id=target, device_id_type=MESH)
            pl.when(slab == n_z - 1)(copy.start)
            late.append((it, lax.rem(slab - i + n_z, n_z) == n_z - 1, copy))
            sends.append((slab == n_z - 1, copy))
        sends += [(None, copy) for copy in peak_copies]

        if it + 1 < ITERS:
            change = forward(jnp.concatenate(rows, axis=0))
        else:
            for copy in warp_copies[-1]:
                copy.wait_recv()
            tout_ref[...] = sum(warp_ref[it, i] for i in range(n_s)) * (1.0 / n_s)
            store_tmpl = pltpu.make_async_copy(tout_ref, tout_hbm, store_sem.at[0])
            store_tmpl.start()
            for when, come, copy in late:
                if when < it:
                    if come is None:
                        copy.wait_recv()
                    else:
                        pl.when(come)(copy.wait_recv)
            for a in range(grid_z):
                steps = [rows_ref[k, a].astype(jnp.float32) * rates[k][None] for k in range(it)]
                for c in range(3):
                    value = ctrl_ref[c, a, :, 0, :]
                    for step in steps:
                        value = value - step[c, :grid_y]
                    base_ref[c, a, :grid_y] = value
        for copy in peak_copies:
            copy.wait_recv()
        top = peak_ref[it, 0]
        for k in range(1, n_z):
            top = jnp.maximum(top, peak_ref[it, k])
        top = jnp.sqrt(jnp.max(top, axis=(0, 1), keepdims=True))
        rates.append(step_length / (top + tiny_term))
        if it + 1 < ITERS:
            xw_ref[...] = xw_ref[...] - change * rates[it][None]

    for when, come, copy in late:
        if when == ITERS - 1:
            if come is None:
                copy.wait_recv()
            else:
                pl.when(come)(copy.wait_recv)
    for a in range(grid_z):
        step = rows_ref[ITERS - 1, a].astype(jnp.float32) * rates[ITERS - 1][None]
        for c in range(3):
            cout_ref[c, a, :, 0, :] = base_ref[c, a, :grid_y] - step[c, :grid_y]
    store_ctrl = pltpu.make_async_copy(cout_ref, cout_hbm, store_sem.at[1])
    store_ctrl.start()
    for go, copy in sends:
        if go is None:
            copy.wait_send()
        else:
            pl.when(go)(copy.wait_send)
    store_tmpl.wait()
    store_ctrl.wait()


def shards(sizes, subjects, offsets, template, control):
    n_z, n_y, n_s = sizes
    depth, height, width = subjects.shape[1:]
    halves = width // LANES
    cells = depth // KNOT
    band = cells + 3
    grid_z = control.shape[2]
    control = control.reshape(control.shape[1:4] + (1, control.shape[4]))
    low, full = jnp.bfloat16, jnp.float32
    dma = pltpu.SemaphoreType.DMA
    scratch = [
        pltpu.VMEM(subjects.shape, low),
        pltpu.VMEM(offsets.shape, offsets.dtype),
        pltpu.VMEM(template.shape, full),
        pltpu.VMEM(control.shape, full),
        pltpu.VMEM(template.shape, full),
        pltpu.VMEM(control.shape, full),
        pltpu.VMEM((3, grid_z, SUB, LANES), full),
        pltpu.VMEM((2, depth, height, width), low),
        pltpu.VMEM((2, 3, HALO, height, width), low),
        pltpu.VMEM((SPAN, halves, depth + 2 * HALO, 3 * SUB, LANES), full),
        pltpu.VMEM((8, depth, height, width), full),
        pltpu.VMEM((band * 3, SUB, width), full),
        pltpu.VMEM((band * 3, SUB, width), full),
        pltpu.VMEM((ITERS, n_y, band, 3, SUB, LANES), low),
        pltpu.VMEM((ITERS, n_y, 3, 3, SUB, LANES), low),
        pltpu.VMEM((ITERS, n_y, 3, 3, SUB, LANES), low),
        pltpu.VMEM((ITERS, grid_z, 3, SUB, LANES), low),
        pltpu.VMEM((ITERS, n_z, SUB, LANES), full),
        pltpu.VMEM((ITERS, n_s, depth, height, width), full),
        dma((2,)), dma((2,)), dma((2, 3)), dma((2, 3)),
        dma((ITERS, n_y)), dma((ITERS, n_y)), dma((ITERS, 2, n_y)), dma((ITERS, 2, n_y)),
        dma((ITERS, n_z)), dma((ITERS, n_z)), dma((ITERS, n_z)), dma((ITERS, n_z)),
        dma((ITERS, n_z)), dma((ITERS, n_z)), dma((ITERS, n_s)), dma((ITERS, n_s)),
        pltpu.SemaphoreType.REGULAR((2,)), dma((4,)), dma((2,)),
    ]
    tmpl, ctrl = pl.pallas_call(
        functools.partial(kernel, sizes),
        out_shape=(
            jax.ShapeDtypeStruct(template.shape, full),
            jax.ShapeDtypeStruct(control.shape, full),
        ),
        in_specs=[pl.BlockSpec(memory_space=pl.ANY)] * 4,
        out_specs=(pl.BlockSpec(memory_space=pl.ANY),) * 2,
        scratch_shapes=scratch,
        compiler_params=pltpu.CompilerParams(collective_id=0, has_side_effects=True),
        name="register",
    )(subjects, offsets, template, control)
    return tmpl, ctrl.reshape((1,) + ctrl.shape[:3] + (ctrl.shape[4],))


def solution(mesh):
    in_specs = (
        P(("group", "subj"), "slab", "yslab", None),
        P(("group", "subj"), None, "slab", "yslab", None),
        P(("group", "slab"), "yslab", None),
        P(("group", "subj"), None, None, None, None),
    )
    out_specs = (P(("group", "slab"), "yslab", None), P(("group", "subj"), None, None, None, None))
    sizes = (mesh.shape["slab"], mesh.shape["yslab"], mesh.shape["subj"])
    body = functools.partial(shards, sizes)
    return jax.shard_map(body, mesh=mesh, in_specs=in_specs, out_specs=out_specs, check_vma=False)
```

```python
import functools

import jax
import jax.numpy as jnp
from jax import lax
from jax.experimental import pallas as pl
from jax.experimental.pallas import tpu as pltpu
from jax.sharding import PartitionSpec as P

KNOT = 4
KNOT_X = 2
HALO = 2
ITERS = 2
SPAN = 2 * HALO + 1
LANES = 128
SUB = 8

step_length = 0.5
tiny_term = 1e-06

MESH = pl.DeviceIdType.MESH


def spline(step, spacing):
    s = step / spacing
    return (
        (1.0 - s) ** 3 / 6.0,
        (3.0 * s**3 - 6.0 * s**2 + 4.0) / 6.0,
        (-3.0 * s**3 + 3.0 * s**2 + 3.0 * s + 1.0) / 6.0,
        s**3 / 6.0,
    )


def spline_table(step, column, spacing, scale):
    out = jnp.zeros(step.shape, jnp.float32)
    for s in range(spacing):
        for k, weight in enumerate(spline(s, spacing)):
            if weight != 0.0:
                out = jnp.where((step == s) & (column == k), jnp.float32(weight * scale), out)
    return out


def pick(values, upper, odd):
    first = jnp.where(upper, values[2], values[0])
    second = jnp.where(upper, values[3], values[1])
    third = jnp.where(upper, values[4], values[2])
    return jnp.where(odd, second, first), jnp.where(odd, third, second)


def split(value):
    high = value.astype(jnp.bfloat16)
    low = (value - high.astype(jnp.float32)).astype(jnp.bfloat16)
    return jnp.concatenate([high, low], axis=1)


def kernel(
    sizes, subj_hbm, off_hbm, tmpl_hbm, ctrl_hbm, tout_ref, cout_ref,
    subj_ref, off_ref, tmpl_ref, ctrl_ref, base_ref,
    side_ref, face_ref, ext_ref, corner_ref, xw_ref, grad_ref, part_ref, below_ref, above_ref,
    rows_ref, peak_ref, warp_ref,
    side_send, side_recv, face_send, face_recv, part_send, part_recv, edge_send, edge_recv,
    rows_send, rows_recv, last_send, last_recv, peak_send, peak_recv, warp_send, warp_recv,
    relay_sem, load_sem,
):
    n_z, n_y, n_s = sizes
    depth, height, width = subj_ref.shape[1:]
    halves = width // LANES
    cells = depth // KNOT
    band = cells + 3
    grid_z, grid_y, grid_x = ctrl_ref.shape[1], ctrl_ref.shape[2], ctrl_ref.shape[4]
    slab = lax.axis_index("slab")
    yslab = lax.axis_index("yslab")
    subj = lax.axis_index("subj")
    first_row = slab * cells

    def inside(dz, dy):
        z, y = slab + dz, yslab + dy
        return (z >= 0) & (z < n_z) & (y >= 0) & (y < n_y)

    barrier = pltpu.get_barrier_semaphore()
    for k in range(1, n_y):
        pl.semaphore_signal(
            barrier, inc=1, device_id={"yslab": lax.rem(yslab + k, n_y)}, device_id_type=MESH
        )
    for i in range(1, n_s):
        pl.semaphore_signal(
            barrier, inc=1, device_id={"subj": lax.rem(subj + i, n_s)}, device_id_type=MESH
        )
    greeted = n_y - 1 + n_s - 1
    for dz in (-1, 1):
        @pl.when(inside(dz, 0))
        def _():
            for k in range(n_y):
                pl.semaphore_signal(
                    barrier, inc=1, device_id_type=MESH,
                    device_id={"slab": slab + dz, "yslab": lax.rem(yslab + k, n_y)},
                )
        greeted = greeted + jnp.where(inside(dz, 0), n_y, 0)

    loads = [
        pltpu.make_async_copy(src, dst, load_sem.at[i])
        for i, (src, dst) in enumerate((
            (subj_hbm, subj_ref), (ctrl_hbm, ctrl_ref), (off_hbm, off_ref), (tmpl_hbm, tmpl_ref)))
    ]
    for load in loads:
        load.start()

    def iota(shape, axis):
        return lax.broadcasted_iota(jnp.int32, shape, axis)

    scale_x = 6.0 * KNOT_X**3

    def x_table(shape, x_axis):
        x, g = iota(shape, x_axis), iota(shape, 1 - x_axis)
        column = g - x // KNOT_X
        column = jnp.where(column < 0, column + grid_x, column)
        return spline_table(x % KNOT_X, column, KNOT_X, scale_x).astype(jnp.bfloat16)

    spread_x = x_table((grid_x, width), 1)
    spread_x = jnp.concatenate([spread_x, spread_x], axis=0)
    gather_x = x_table((width, grid_x), 0)
    gather_x = jnp.concatenate([gather_x, gather_x], axis=0)

    def y_weights(y, b):
        column = b - (yslab * height + y) // KNOT
        return spline_table(y % KNOT, column, KNOT, 1.0 / scale_x)

    rows8 = iota((SUB, LANES), 0)
    spread_y = [y_weights(rows8, (rows8 - d) % SUB) for d in range(SUB)]
    gather_y = [y_weights((rows8 - d) % SUB, rows8) for d in range(SUB)]

    def turn(value, weights):
        total = value * weights[0][None]
        for d in range(1, SUB):
            total = total + pltpu.roll(value, d, 1) * weights[d][None]
        return total

    def forward(tiles):
        mixed = turn(tiles, spread_y).reshape(band * 3 * SUB, LANES)
        out = jnp.dot(split(mixed), spread_x, preferred_element_type=jnp.float32)
        return out.reshape(band * 3, SUB, width)

    def adjoint(tiles):
        out = jnp.dot(
            split(tiles.reshape(band * 3 * SUB, width)), gather_x, preferred_element_type=jnp.float32
        )
        return turn(out.reshape(band * 3, SUB, LANES), gather_y)

    @pl.when(slab == 0)
    def _():
        below_ref[...] = jnp.zeros_like(below_ref)

    @pl.when(slab == n_z - 1)
    def _():
        above_ref[...] = jnp.zeros_like(above_ref)

    loads[0].wait()
    pl.semaphore_wait(barrier, greeted)

    def relay_signal():
        for d, dz in enumerate((-1, 1)):
            @pl.when(inside(dz, 0))
            def _():
                pl.semaphore_signal(
                    relay_sem.at[d], inc=1, device_id={"slab": slab + dz}, device_id_type=MESH
                )

    def relay_wait():
        for d, dz in enumerate((1, -1)):
            @pl.when(inside(dz, 0))
            def _():
                pl.semaphore_wait(relay_sem.at[d], 1)

    moves = []
    for dy in (-1, 1):
        moves.append((0, dy, pltpu.make_async_remote_copy(
            src_ref=subj_ref.at[0], dst_ref=side_ref.at[(1 - dy) // 2],
            send_sem=side_send.at[(1 - dy) // 2], recv_sem=side_recv.at[(1 - dy) // 2],
            device_id={"yslab": yslab + dy}, device_id_type=MESH)))
    for dz in (-1, 1):
        start = 0 if dz < 0 else depth - HALO
        for dy in (-1, 0, 1):
            a, b = (1 - dz) // 2, 1 - dy
            moves.append((dz, dy, pltpu.make_async_remote_copy(
                src_ref=subj_ref.at[0, pl.ds(start, HALO)], dst_ref=face_ref.at[a, b],
                send_sem=face_send.at[a, b], recv_sem=face_recv.at[a, b],
                device_id={"slab": slab + dz, "yslab": yslab + dy}, device_id_type=MESH)))
    for dz, dy, copy in moves:
        pl.when(inside(dz, dy))(copy.start)
    if n_z > 2:
        relay_signal()
    loads[1].wait()

    pad = jnp.zeros((SUB - grid_y, LANES), jnp.float32)
    tiles = jnp.stack([
        jnp.concatenate([ctrl_ref[c, first_row + a, :, 0, :], pad], axis=0)
        for a in range(band) for c in range(3)
    ])
    xw_ref[...] = forward(tiles)

    lane = iota((1, SUB, LANES), 2)

    def place(z, tile, block):
        planes = block.shape[0]
        parts = [block[:, :, h * LANES:(h + 1) * LANES] for h in range(halves)]
        zero = jnp.zeros_like(parts[0])
        for dx in range(-HALO, HALO + 1):
            if dx == 0:
                moved = parts
            else:
                rolled = [pltpu.roll(p, (-dx) % LANES, 2) for p in parts]
                moved = []
                for h in range(halves):
                    other = h + (1 if dx > 0 else -1)
                    fill = rolled[other] if 0 <= other < halves else zero
                    edge = lane >= LANES - dx if dx > 0 else lane < -dx
                    moved.append(jnp.where(edge, fill, rolled[h]))
            for h in range(halves):
                ext_ref[dx + HALO, h, pl.ds(z, planes), tile * SUB:(tile + 1) * SUB, :] = moved[h]

    own = 4

    def place_many(tile, load):
        def body(i, carry):
            place(HALO + i * own, tile, load(pl.ds(i * own, own)).astype(jnp.float32))
            return carry
        lax.fori_loop(0, depth // own, body, 0)

    place_many(1, lambda part: subj_ref[0, part])

    for dz, dy, copy in moves:
        if dz == 0:
            pl.when(inside(-dz, -dy))(copy.wait_recv)
    for d, dy in enumerate((-1, 1)):
        tile = 1 + dy

        @pl.when(inside(0, dy))
        def _():
            place_many(tile, lambda part: side_ref[d, part])

        @pl.when(jnp.logical_not(inside(0, dy)))
        def _():
            ext_ref[:, :, :, tile * SUB:(tile + 1) * SUB, :] = jnp.zeros(
                (SPAN, halves, depth + 2 * HALO, SUB, LANES), jnp.float32)
    def corners(z, carry):
        for h in range(halves):
            cut = slice(h * LANES, (h + 1) * LANES)
            bits = [(off_ref[0, i, z, :, cut] >= 0, (off_ref[0, i, z, :, cut] & 1) == 1) for i in range(3)]
            by_z = []
            for dz in range(SPAN):
                by_y = []
                for dy in range(SPAN):
                    start = SUB - HALO + dy
                    row = [ext_ref[dx, h, z + dz, start:start + SUB, :] for dx in range(SPAN)]
                    by_y.append(pick(row, *bits[2]))
                by_z.append([pick([v[x] for v in by_y], *bits[1]) for x in range(2)])
            for x in range(2):
                for y in range(2):
                    low, high = pick([v[x][y] for v in by_z], *bits[0])
                    corner_ref[0 + 2 * y + x, z, :, cut] = low
                    corner_ref[4 + 2 * y + x, z, :, cut] = high
        return carry

    loads[2].wait()
    lax.fori_loop(HALO, depth - HALO, corners, 0)
    for dz, dy, copy in moves:
        if dz != 0:
            pl.when(inside(-dz, -dy))(copy.wait_recv)
    for a, dz in enumerate((-1, 1)):
        z = 0 if dz < 0 else depth + HALO
        for b, dy in enumerate((-1, 0, 1)):
            @pl.when(inside(dz, dy))
            def _():
                place(z, b, face_ref[a, b].astype(jnp.float32))

            @pl.when(jnp.logical_not(inside(dz, dy)))
            def _():
                ext_ref[:, :, z:z + HALO, b * SUB:(b + 1) * SUB, :] = jnp.zeros(
                    (SPAN, halves, HALO, SUB, LANES), jnp.float32)
    lax.fori_loop(0, HALO, corners, 0)
    lax.fori_loop(depth - HALO, depth, corners, 0)
    for _ in range(2, n_z - 1):
        relay_wait()
        relay_signal()
    loads[3].wait()

    weights_z = [spline(s, KNOT) for s in range(KNOT)]
    sends = [(inside(dz, dy), copy) for dz, dy, copy in moves]
    late = []
    warp_copies = []
    rates = []

    for it in range(ITERS):
        grad_ref[...] = jnp.zeros_like(grad_ref)
        if it > 0:
            for copy in warp_copies[-1]:
                copy.wait_recv()

        def cell(j, carry):
            for h in range(halves):
                cut = slice(h * LANES, (h + 1) * LANES)
                knots = [[xw_ref[(j + k) * 3 + c, :, cut] for k in range(4)] for c in range(3)]
                sums = [[None] * 4 for _ in range(3)]
                for s in range(KNOT):
                    z = j * KNOT + s
                    used = [k for k in range(4) if weights_z[s][k] != 0.0]
                    th, f = [], []
                    for c in range(3):
                        u = sum(knots[c][k] * weights_z[s][k] for k in used)
                        th.append(jnp.tanh(u))
                        f.append(0.5 + 0.5 * th[c])
                    v = [corner_ref[i, z, :, cut] for i in range(8)]
                    dx = [v[2 * i + 1] - v[2 * i] for i in range(4)]
                    ax = [v[2 * i] + dx[i] * f[2] for i in range(4)]
                    dy = [ax[1] - ax[0], ax[3] - ax[2]]
                    ay = [ax[0] + dy[0] * f[1], ax[2] + dy[1] * f[1]]
                    dxy = [dx[0] + (dx[1] - dx[0]) * f[1], dx[2] + (dx[3] - dx[2]) * f[1]]
                    slope_z = ay[1] - ay[0]
                    warped = ay[0] + slope_z * f[0]
                    slope_y = dy[0] + (dy[1] - dy[0]) * f[0]
                    slope_x = dxy[0] + (dxy[1] - dxy[0]) * f[0]
                    warp_ref[it, subj, z, :, cut] = warped
                    if it == 0:
                        current = tmpl_ref[z, :, cut]
                    else:
                        current = sum(warp_ref[it - 1, i, z, :, cut] for i in range(n_s)) * (1.0 / n_s)
                    resid = warped - current
                    for c, slope in enumerate((slope_z, slope_y, slope_x)):
                        g = resid * slope * (1.0 - th[c] * th[c])
                        for k in used:
                            term = g * weights_z[s][k]
                            sums[c][k] = term if sums[c][k] is None else sums[c][k] + term
                for c in range(3):
                    for k in range(4):
                        grad_ref[(j + k) * 3 + c, :, cut] += sums[c][k]
            return carry

        lax.fori_loop(0, cells, cell, 0)

        copies = []
        for i in range(1, n_s):
            copy = pltpu.make_async_remote_copy(
                src_ref=warp_ref.at[it, subj], dst_ref=warp_ref.at[it, subj],
                send_sem=warp_send.at[it, i], recv_sem=warp_recv.at[it, i],
                device_id={"subj": lax.rem(subj + i, n_s)}, device_id_type=MESH)
            copies.append(copy)
        warp_copies.append(copies)

        part = adjoint(grad_ref[...])
        part_ref[it, yslab] = part.reshape(band, 3, SUB, LANES).astype(jnp.bfloat16)

        part_copies = []
        for i in range(1, n_y):
            copy = pltpu.make_async_remote_copy(
                src_ref=part_ref.at[it, yslab], dst_ref=part_ref.at[it, yslab],
                send_sem=part_send.at[it, i], recv_sem=part_recv.at[it, i],
                device_id={"yslab": lax.rem(yslab + i, n_y)}, device_id_type=MESH)
            part_copies.append(copy)
        edge_copies = []
        for e, dz in enumerate((1, -1)):
            landing = below_ref if dz > 0 else above_ref
            start = cells if dz > 0 else 0
            for i in range(n_y):
                copy = pltpu.make_async_remote_copy(
                    src_ref=part_ref.at[it, yslab, pl.ds(start, 3)], dst_ref=landing.at[it, yslab],
                    send_sem=edge_send.at[it, e, i], recv_sem=edge_recv.at[it, e, i],
                    device_id={"slab": slab + dz, "yslab": lax.rem(yslab + i, n_y)},
                    device_id_type=MESH)
                edge_copies.append((inside(dz, 0), inside(-dz, 0), copy))
        for go, _, copy in edge_copies:
            pl.when(go)(copy.start)
        for copy in part_copies:
            copy.start()
        for copy in copies:
            copy.start()
        for copy in part_copies:
            copy.wait_recv()
        for _, come, copy in edge_copies:
            pl.when(come)(copy.wait_recv)
        sends += [(go, copy) for go, _, copy in edge_copies]
        sends += [(None, copy) for copy in part_copies + copies]

        def over_y(ref, where):
            return sum(ref[it, k, where].astype(jnp.float32) for k in range(n_y))

        rows = []
        for a in range(band):
            row = over_y(part_ref, a)
            if a < 3:
                row = row + over_y(below_ref, a)
            if a >= cells:
                row = row + over_y(above_ref, a - cells)
            rows.append(row)
        square = None
        for row in rows:
            here = row[0] * row[0] + row[1] * row[1] + row[2] * row[2]
            square = here if square is None else jnp.maximum(square, here)
        for d in (1, 2, 4):
            square = jnp.maximum(square, pltpu.roll(square, d, 0))
        peak_ref[it, slab] = square[:1]
        if it == 0 and n_z > 2:
            relay_wait()
        peak_copies = []
        for i in range(1, n_z):
            copy = pltpu.make_async_remote_copy(
                src_ref=peak_ref.at[it, slab], dst_ref=peak_ref.at[it, slab],
                send_sem=peak_send.at[it, i], recv_sem=peak_recv.at[it, i],
                device_id={"slab": lax.rem(slab + i, n_z)}, device_id_type=MESH)
            peak_copies.append(copy)
        for a in range(cells):
            rows_ref[it, first_row + a] = rows[a].astype(jnp.bfloat16)

        @pl.when(slab == n_z - 1)
        def _():
            for a in range(cells, band):
                rows_ref[it, first_row + a] = rows[a].astype(jnp.bfloat16)

        for copy in peak_copies:
            copy.start()
        last = n_z * cells
        for i in range(1, n_z):
            target = {"slab": lax.rem(slab + i, n_z)}
            own_rows = rows_ref.at[it, pl.ds(first_row, cells)]
            copy = pltpu.make_async_remote_copy(
                src_ref=own_rows, dst_ref=own_rows,
                send_sem=rows_send.at[it, i], recv_sem=rows_recv.at[it, i],
                device_id=target, device_id_type=MESH)
            copy.start()
            late.append((it, None, copy))
            sends.append((None, copy))
            last_rows = rows_ref.at[it, pl.ds(last, 3)]
            copy = pltpu.make_async_remote_copy(
                src_ref=last_rows, dst_ref=last_rows,
                send_sem=last_send.at[it, i], recv_sem=last_recv.at[it, i],
                device_id=target, device_id_type=MESH)
            pl.when(slab == n_z - 1)(copy.start)
            late.append((it, lax.rem(slab - i + n_z, n_z) == n_z - 1, copy))
            sends.append((slab == n_z - 1, copy))
        sends += [(None, copy) for copy in peak_copies]

        if it + 1 < ITERS:
            change = forward(jnp.concatenate(rows, axis=0))
        else:
            for copy in warp_copies[-1]:
                copy.wait_recv()
            tout_ref[...] = sum(warp_ref[it, i] for i in range(n_s)) * (1.0 / n_s)
            for when, come, copy in late:
                if when < it:
                    if come is None:
                        copy.wait_recv()
                    else:
                        pl.when(come)(copy.wait_recv)
            for a in range(grid_z):
                steps = [rows_ref[k, a].astype(jnp.float32) * rates[k][None] for k in range(it)]
                for c in range(3):
                    value = ctrl_ref[c, a, :, 0, :]
                    for step in steps:
                        value = value - step[c, :grid_y]
                    base_ref[c, a, :grid_y] = value
        for copy in peak_copies:
            copy.wait_recv()
        top = peak_ref[it, 0]
        for k in range(1, n_z):
            top = jnp.maximum(top, peak_ref[it, k])
        top = jnp.sqrt(jnp.max(top, axis=(0, 1), keepdims=True))
        rates.append(step_length / (top + tiny_term))
        if it + 1 < ITERS:
            xw_ref[...] = xw_ref[...] - change * rates[it][None]

    for when, come, copy in late:
        if when == ITERS - 1:
            if come is None:
                copy.wait_recv()
            else:
                pl.when(come)(copy.wait_recv)
    for a in range(grid_z):
        step = rows_ref[ITERS - 1, a].astype(jnp.float32) * rates[ITERS - 1][None]
        for c in range(3):
            cout_ref[c, a, :, 0, :] = base_ref[c, a, :grid_y] - step[c, :grid_y]
    for go, copy in sends:
        if go is None:
            copy.wait_send()
        else:
            pl.when(go)(copy.wait_send)


def shards(sizes, subjects, offsets, template, control):
    n_z, n_y, n_s = sizes
    depth, height, width = subjects.shape[1:]
    halves = width // LANES
    cells = depth // KNOT
    band = cells + 3
    grid_z = control.shape[2]
    control = control.reshape(control.shape[1:4] + (1, control.shape[4]))
    low, full = jnp.bfloat16, jnp.float32
    dma = pltpu.SemaphoreType.DMA
    scratch = [
        pltpu.VMEM(subjects.shape, low),
        pltpu.VMEM(offsets.shape, offsets.dtype),
        pltpu.VMEM(template.shape, full),
        pltpu.VMEM(control.shape, full),
        pltpu.VMEM((3, grid_z, SUB, LANES), full),
        pltpu.VMEM((2, depth, height, width), low),
        pltpu.VMEM((2, 3, HALO, height, width), low),
        pltpu.VMEM((SPAN, halves, depth + 2 * HALO, 3 * SUB, LANES), full),
        pltpu.VMEM((8, depth, height, width), full),
        pltpu.VMEM((band * 3, SUB, width), full),
        pltpu.VMEM((band * 3, SUB, width), full),
        pltpu.VMEM((ITERS, n_y, band, 3, SUB, LANES), low),
        pltpu.VMEM((ITERS, n_y, 3, 3, SUB, LANES), low),
        pltpu.VMEM((ITERS, n_y, 3, 3, SUB, LANES), low),
        pltpu.VMEM((ITERS, grid_z, 3, SUB, LANES), low),
        pltpu.VMEM((ITERS, n_z, 1, LANES), full),
        pltpu.VMEM((ITERS, n_s, depth, height, width), full),
        dma((2,)), dma((2,)), dma((2, 3)), dma((2, 3)),
        dma((ITERS, n_y)), dma((ITERS, n_y)), dma((ITERS, 2, n_y)), dma((ITERS, 2, n_y)),
        dma((ITERS, n_z)), dma((ITERS, n_z)), dma((ITERS, n_z)), dma((ITERS, n_z)),
        dma((ITERS, n_z)), dma((ITERS, n_z)), dma((ITERS, n_s)), dma((ITERS, n_s)),
        pltpu.SemaphoreType.REGULAR((2,)), dma((4,)),
    ]
    tmpl, ctrl = pl.pallas_call(
        functools.partial(kernel, sizes),
        out_shape=(
            pltpu.VMEM(template.shape, full),
            pltpu.VMEM(control.shape, full),
        ),
        in_specs=[pl.BlockSpec(memory_space=pl.ANY)] * 4,
        out_specs=(pl.BlockSpec(memory_space=pltpu.VMEM),) * 2,
        scratch_shapes=scratch,
        compiler_params=pltpu.CompilerParams(collective_id=0, has_side_effects=True),
        name="register",
    )(subjects, offsets, template, control)
    return tmpl, ctrl.reshape((1,) + ctrl.shape[:3] + (ctrl.shape[4],))


def solution(mesh):
    in_specs = (
        P(("group", "subj"), "slab", "yslab", None),
        P(("group", "subj"), None, "slab", "yslab", None),
        P(("group", "slab"), "yslab", None),
        P(("group", "subj"), None, None, None, None),
    )
    out_specs = (P(("group", "slab"), "yslab", None), P(("group", "subj"), None, None, None, None))
    sizes = (mesh.shape["slab"], mesh.shape["yslab"], mesh.shape["subj"])
    body = functools.partial(shards, sizes)
    return jax.shard_map(body, mesh=mesh, in_specs=in_specs, out_specs=out_specs, check_vma=False)
```
